256 devices in a mesh: group: 16 (over z, core), dev: 16 (over y, x).
Axes of the slice: x: 4, y: 4, z: 8, core: 2. Of those that a mesh axis runs over, the one named last changes fastest.
Arguments:
- tokens: bfloat16 [1024, 7168], P(('group', 'dev')), may hold values from -6 to 6
- group_ids: int32 [1024, 4], P(('group', 'dev')), may hold values from 0 to 15, as said below
- expert_ids: int32 [1024, 8], P(('group', 'dev')), may hold values from 0 to 63, as said below
- gate_scores: bfloat16 [1024, 8], P(('group', 'dev')), may hold values from 0.099609375 to 1
- w_gate: bfloat16 [7168, 65536], P(None, ('group', 'dev')), may hold values from -0.0625 to 0.0625
- w_up: bfloat16 [7168, 65536], P(None, ('group', 'dev')), may hold values from -0.0625 to 0.0625
- w_down: bfloat16 [65536, 7168], P(('group', 'dev')), may hold values from -0.1875 to 0.1875
Outputs:
- combined: bfloat16 [1024, 7168], P(('group', 'dev'))
The draws below stay inside these ranges and needn't reach their ends.
Inputs may be any that keep to these rules, and one draw needn't show every extreme that they name: `group_ids`: each row names 4 different groups; among the 4 rows of one aligned block, at most 2 rows name any one group. `expert_ids`: each row names 8 different experts, exactly two in each group of the row's group_ids (expert x lies in group x // 4).
All inputs are finite; a program needn't handle non-finite values.
Results may differ from the reference program's by a relative error of at most 0.014.
Values may be sent and summed in bfloat16 or wider, within the bound.
No kernel may reach another device: no remote copies, remote signals or barrier semaphores. Data moves between devices by JAX's collectives and lax.ppermute only.
A program may use at most 64 MiB of HBM per device.

```python
import math
import jax
import jax.numpy as jnp
from jax import lax

D = 7168
FF = 1024
EXP_GROUP = 4
TOPG = 4
TOPK = 8
TOK_DEV = 4
CAP = 2
GROUPS = 16
BLOCKS = 256
EXPERTS = 64
TOKENS = 1024
FC = 256
N_GROUP = 16


def route_plan(key):
    base_key = jax.random.fold_in(key, 11)
    favored = jax.random.randint(jax.random.fold_in(base_key, 1), (), 0, GROUPS).astype(jnp.int32)
    order_keys = jax.random.split(jax.random.fold_in(base_key, 2), BLOCKS)
    group_orders = jax.vmap(lambda block_key: jax.random.permutation(block_key, GROUPS))(order_keys).astype(jnp.int32)
    fav_last = jnp.argsort((group_orders == favored).astype(jnp.int32), axis=1, stable=True)
    other_groups = jnp.take_along_axis(group_orders, fav_last, axis=1)[:, :GROUPS - 1]
    remaining = TOK_DEV * TOPG - CAP
    least_active = (remaining + CAP - 1) // CAP
    active_count = jax.random.randint(jax.random.fold_in(base_key, 8), (BLOCKS, 1, 1), least_active, GROUPS).astype(jnp.int32)
    offset_draw = jax.random.randint(jax.random.fold_in(base_key, 3), (BLOCKS, 1, 1), 0, GROUPS - 1).astype(jnp.int32)
    token_pos = jnp.arange(TOK_DEV, dtype=jnp.int32)[:, None]
    choice_pos = jnp.arange(TOPG, dtype=jnp.int32)[None, :]
    is_hot = token_pos < CAP
    other_slot = token_pos * TOPG - jnp.minimum(token_pos, CAP) + choice_pos - is_hot.astype(jnp.int32)
    cyclic_index = (other_slot[None] + offset_draw) % active_count
    block_iota = jnp.arange(BLOCKS, dtype=jnp.int32)
    chosen = other_groups[block_iota[:, None, None], cyclic_index]
    chosen = jnp.where((is_hot & (choice_pos == 0))[None], favored, chosen)
    rotation = jax.random.randint(jax.random.fold_in(base_key, 4), (BLOCKS, TOK_DEV, 1), 0, TOPG).astype(jnp.int32)
    rotated_pos = (choice_pos[None] + rotation) % TOPG
    chosen = jnp.take_along_axis(chosen, rotated_pos, axis=2)
    token_keys = jax.random.split(jax.random.fold_in(base_key, 5), BLOCKS)
    token_order = jax.vmap(lambda block_key: jax.random.permutation(block_key, TOK_DEV))(token_keys).astype(jnp.int32)
    chosen = chosen[block_iota[:, None], token_order]
    first_expert = jax.random.randint(jax.random.fold_in(base_key, 6), (BLOCKS, TOK_DEV, TOPG), 0, EXP_GROUP).astype(jnp.int32)
    expert_step = jax.random.randint(jax.random.fold_in(base_key, 7), (BLOCKS, TOK_DEV, TOPG), 1, EXP_GROUP).astype(jnp.int32)
    second_expert = (first_expert + expert_step) % EXP_GROUP
    experts = jnp.stack([chosen * EXP_GROUP + first_expert, chosen * EXP_GROUP + second_expert], axis=3)
    return (chosen.reshape(TOKENS, TOPG).astype(jnp.int32), experts.reshape(TOKENS, TOPK).astype(jnp.int32))


def draw_group_ids(key, part):
    return route_plan(key)[0]


def draw_expert_ids(key, part):
    return route_plan(key)[1]


def steps_of(key, shape, cuts, least, high):
    def one(position, blocks):
        heights = jax.random.uniform(jax.random.fold_in(jax.random.fold_in(key, 6), position), (blocks,), jnp.float32, least / len(cuts), high / len(cuts))
        return jnp.repeat(jnp.exp(heights), shape[position] // blocks).reshape((-1,) + (1,) * (len(shape) - position - 1))

    loudness = one(*cuts[0])
    for cut in cuts[1:]:
        loudness = loudness * one(*cut)
    return loudness


def scatter_about(key, dims, scale, most, shards=(), kind=jnp.bfloat16):
    result = jax.random.normal(key, dims, jnp.float32) * scale
    if len(shards) > 0:
        result = steps_of(key, dims, shards, -0.22, 0.18) * result
    return jnp.clip(result, min=-most, max=most).astype(kind)


def setup_inputs(seed: int = 0) -> dict:
    splits = jax.random.split(jax.random.key(seed), 8)
    return {
        "tokens": scatter_about(splits[0], (TOKENS, D), 1.0, 6.0, ((0, 256),)),
        "group_ids": draw_group_ids(jax.random.fold_in(splits[7], 71), 0),
        "expert_ids": draw_expert_ids(jax.random.fold_in(splits[7], 71), 0),
        "gate_scores": jnp.clip(jnp.exp(math.log(1.0) - 2.306499 * jax.random.uniform(splits[3], (TOKENS, TOPK), jnp.float32) ** steps_of(splits[3], (TOKENS, TOPK), ((0, 256),), -0.2, 0.2)), 0.099609375, 1.0).astype(jnp.bfloat16),
        "w_gate": scatter_about(splits[4], (D, EXPERTS * FF), D ** -0.5, 0.0625, ((1, 256),)),
        "w_up": scatter_about(splits[5], (D, EXPERTS * FF), D ** -0.5, 0.0625, ((1, 256),)),
        "w_down": scatter_about(splits[6], (EXPERTS * FF, D), FF ** -0.5, 0.1875, ((0, 256),)),
    }


def reference(tokens, group_ids, expert_ids, gate_scores, w_gate, w_up, w_down):
    block_total = TOKENS // TOK_DEV
    activations = tokens.astype(jnp.float32).reshape(block_total, TOK_DEV, D)
    group_sel = group_ids.reshape(block_total, TOK_DEV, TOPG)
    expert_sel = expert_ids.reshape(block_total, TOK_DEV, TOPK)
    scores = gate_scores.astype(jnp.float32).reshape(block_total, TOK_DEV, TOPK)
    group_span = EXP_GROUP * FF
    column_blocks = group_span // FC
    slot_iota = jnp.arange(CAP, dtype=jnp.int32)
    expert_iota = jnp.arange(EXP_GROUP, dtype=jnp.int32)
    highest = lax.Precision.HIGHEST

    def per_group(running, group_index):
        member = jnp.sum((group_sel == group_index).astype(jnp.int32), axis=2)
        before = jnp.cumsum(member, axis=1) - member
        select = ((member[:, None, :] == 1) & (before[:, None, :] == slot_iota[None, :, None])).astype(jnp.float32)
        row_block = jnp.einsum("bst,btd->bsd", select, activations, precision=highest).reshape(-1, D)
        matches = (expert_sel[:, :, :, None] == group_index * EXP_GROUP + expert_iota).astype(jnp.float32)
        coef = jnp.sum(scores[..., None] * matches, axis=2)
        coef_rows = jnp.einsum("bst,bte->bse", select, coef, precision=highest).reshape(-1, EXP_GROUP)
        gate_group = lax.dynamic_slice_in_dim(w_gate, group_index * group_span, group_span, 1)
        up_group = lax.dynamic_slice_in_dim(w_up, group_index * group_span, group_span, 1)
        down_group = lax.dynamic_slice_in_dim(w_down, group_index * group_span, group_span, 0)

        def per_block(summed, block_index):
            col_start = block_index * FC
            gate_cols = lax.dynamic_slice_in_dim(gate_group, col_start, FC, 1).astype(jnp.float32)
            up_cols = lax.dynamic_slice_in_dim(up_group, col_start, FC, 1).astype(jnp.float32)
            down_rows = lax.dynamic_slice_in_dim(down_group, col_start, FC, 0).astype(jnp.float32)
            owner_expert = (col_start + jnp.arange(FC, dtype=jnp.int32)) // FF
            onehot = (owner_expert[None, :] == expert_iota[:, None]).astype(jnp.float32)
            col_scale = jnp.dot(coef_rows, onehot, precision=highest)
            gate_out = jnp.dot(row_block, gate_cols, precision=highest)
            up_out = jnp.dot(row_block, up_cols, precision=highest)
            hidden = (col_scale * jax.nn.silu(gate_out) * up_out).astype(jnp.bfloat16)
            partial_value = jnp.dot(hidden.astype(jnp.float32), down_rows, precision=highest).astype(jnp.bfloat16)
            partial_value = lax.optimization_barrier(partial_value)
            return summed + partial_value.astype(jnp.float32), None

        summed, _ = lax.scan(per_block, jnp.zeros((block_total * CAP, D), jnp.float32), jnp.arange(column_blocks, dtype=jnp.int32))
        group_out = lax.optimization_barrier(summed.astype(jnp.bfloat16))
        group_out = group_out.astype(jnp.float32).reshape(block_total, CAP, D)
        back_rows = jnp.einsum("bst,bsd->btd", select, group_out, precision=highest)
        return running + back_rows, None

    running, _ = lax.scan(per_group, jnp.zeros((block_total, TOK_DEV, D), jnp.float32), jnp.arange(N_GROUP, dtype=jnp.int32))
    return running.reshape(TOKENS, D).astype(jnp.bfloat16)
```

```python
import jax
import jax.numpy as jnp
from jax import lax
from jax.sharding import PartitionSpec as P

FF = 1024
EXP_GROUP = 4
CAP = 2


def local(tokens, group_ids, expert_ids, gate_scores, w_gate, w_up, w_down):
    group_count = lax.axis_size("group")
    dev_count = lax.axis_size("dev")
    model_width = tokens.shape[1]
    block_cols = w_gate.shape[1]
    expert_total = group_count * EXP_GROUP
    group_iota = jnp.arange(group_count, dtype=jnp.int32)
    member = jnp.sum((group_ids[:, :, None] == group_iota[None, None, :]).astype(jnp.int32), axis=1)
    before = jnp.cumsum(member, axis=0) - member
    slot_iota = jnp.arange(CAP, dtype=jnp.int32)
    select = (member.T[:, None, :] == 1) & (before.T[:, None, :] == slot_iota[None, :, None])
    select_rows = select.astype(jnp.bfloat16)
    matches = (
        expert_ids[:, :, None] == jnp.arange(expert_total, dtype=jnp.int32)[None, None, :]
    ).astype(jnp.float32)
    coef = jnp.sum(gate_scores.astype(jnp.float32)[:, :, None] * matches, axis=1)
    coef = coef.reshape(-1, group_count, EXP_GROUP).astype(jnp.bfloat16)
    send_rows = jnp.einsum(
        "gst,td->gsd", select_rows, tokens, preferred_element_type=jnp.float32
    ).astype(jnp.bfloat16)
    send_coef = jnp.einsum(
        "gst,tge->gse", select_rows, coef, preferred_element_type=jnp.float32
    ).astype(jnp.bfloat16)
    recv_rows, recv_coef = (
        lax.all_to_all(send_rows, "group", split_axis=0, concat_axis=0, tiled=True),
        lax.all_to_all(send_coef, "group", split_axis=0, concat_axis=0, tiled=True),
    )
    all_rows, all_coef = (
        lax.all_gather(recv_rows.reshape(-1, model_width), "dev", axis=0, tiled=True),
        lax.all_gather(recv_coef, "dev", axis=0, tiled=True),
    )
    flat_rows = all_rows
    flat_coef = all_coef.reshape(-1, EXP_GROUP)
    dev_index = lax.axis_index("dev")
    owner_expert = (dev_index * block_cols + jnp.arange(block_cols, dtype=jnp.int32)) // FF
    onehot = (owner_expert[None, :] == jnp.arange(EXP_GROUP, dtype=jnp.int32)[:, None]).astype(
        jnp.bfloat16
    )
    gate_out = jnp.dot(flat_rows, w_gate, preferred_element_type=jnp.float32)
    up_out = jnp.dot(flat_rows, w_up, preferred_element_type=jnp.float32)
    col_scale = jnp.dot(flat_coef, onehot, preferred_element_type=jnp.float32)
    hidden = (col_scale * jax.nn.silu(gate_out) * up_out).astype(jnp.bfloat16)
    partial_value = lax.optimization_barrier(
        jnp.dot(hidden, w_down, preferred_element_type=jnp.float32).astype(jnp.bfloat16)
    )
    summed = lax.psum_scatter(partial_value, "dev", scatter_dimension=0, tiled=True)
    returned = lax.all_to_all(
        summed.reshape(group_count, CAP, model_width), "group", split_axis=0, concat_axis=0, tiled=True
    )
    combined = jnp.einsum("gst,gsd->td", select_rows, returned, preferred_element_type=jnp.float32)
    return combined.astype(jnp.bfloat16)


def solution(mesh):
    return jax.shard_map(
        local,
        mesh=mesh,
        in_specs=(
            P(("group", "dev"), None),
            P(("group", "dev"), None),
            P(("group", "dev"), None),
            P(("group", "dev"), None),
            P(None, ("group", "dev")),
            P(None, ("group", "dev")),
            P(("group", "dev"), None),
        ),
        out_specs=P(("group", "dev"), None),
        check_vma=False,
    )
```
